32 devices in a mesh: dp: 4 (over z), fsdp: 8 (over y, x, core).
Axes of the slice: x: 2, y: 2, z: 4, core: 2. Of those that a mesh axis runs over, the one named last changes fastest.
Arguments:
- tokens: bfloat16 [8192, 768], P(('dp', 'fsdp')), may hold values from -6 to 6
- cotangent: bfloat16 [8192, 768], P(('dp', 'fsdp')), may hold values from -6 to 6
- routes: int32 [64, 2], P(('dp', 'fsdp')), may hold values from 0 to 15, as said below
- lengths: int32 [64, 3], P(('dp', 'fsdp')), may hold values from 1 to 64, 128 in all within a row
- buckets: int32 [255], replicated, may hold values from 0 to 511
- w_query: bfloat16 [768, 768], P(('dp', 'fsdp')), may hold values from -0.21875 to 0.21875
- w_key: bfloat16 [768, 768], P(('dp', 'fsdp')), may hold values from -0.21875 to 0.21875
- w_value: bfloat16 [768, 768], P(('dp', 'fsdp')), may hold values from -0.21875 to 0.21875
- w_output: bfloat16 [768, 768], P(('dp', 'fsdp')), may hold values from -1.25 to 1.25
- w_inner: bfloat16 [768, 3072], P(('dp', 'fsdp')), may hold values from -0.21875 to 0.21875
- w_outer: bfloat16 [3072, 768], P(('dp', 'fsdp')), may hold values from -0.109375 to 0.109375
- relative: bfloat16 [512, 768], P(('dp', 'fsdp')), may hold values from -6 to 6
- b_query: bfloat16 [768], P(('dp', 'fsdp')), may hold values from -0.59765625 to 0.59765625
- b_key: bfloat16 [768], P(('dp', 'fsdp')), may hold values from -0.59765625 to 0.59765625
- b_value: bfloat16 [768], P(('dp', 'fsdp')), may hold values from -0.59765625 to 0.59765625
- b_output: bfloat16 [768], P(('dp', 'fsdp')), may hold values from -0.59765625 to 0.59765625
- b_inner: bfloat16 [3072], P(('dp', 'fsdp')), may hold values from -0.59765625 to 0.59765625
- b_outer: bfloat16 [768], P(('dp', 'fsdp')), may hold values from -0.59765625 to 0.59765625
- attn_gain: bfloat16 [768], P(('dp', 'fsdp')), may hold values from 0.5 to 1.5
- attn_shift: bfloat16 [768], P(('dp', 'fsdp')), may hold values from -0.59765625 to 0.59765625
- ffn_gain: bfloat16 [768], P(('dp', 'fsdp')), may hold values from 0.5 to 1.5
- ffn_shift: bfloat16 [768], P(('dp', 'fsdp')), may hold values from -0.59765625 to 0.59765625
- rel_gain: bfloat16 [768], P(('dp', 'fsdp')), may hold values from 0.5 to 1.5
- rel_shift: bfloat16 [768], P(('dp', 'fsdp')), may hold values from -0.59765625 to 0.59765625
Outputs:
- output: bfloat16 [8192, 768], P(('dp', 'fsdp'))
- grad_input: bfloat16 [8192, 768], P(('dp', 'fsdp'))
- grad_w_query: float32 [768, 768], P(('dp', 'fsdp'))
- grad_w_key: float32 [768, 768], P(('dp', 'fsdp'))
- grad_w_value: float32 [768, 768], P(('dp', 'fsdp'))
- grad_w_output: float32 [768, 768], P(('dp', 'fsdp'))
- grad_w_inner: float32 [768, 3072], P(('dp', 'fsdp'))
- grad_w_outer: float32 [3072, 768], P(('dp', 'fsdp'))
- grad_relative: float32 [512, 768], P(('dp', 'fsdp'))
- grad_b_query: float32 [768], P(('dp', 'fsdp'))
- grad_b_key: float32 [768], P(('dp', 'fsdp'))
- grad_b_value: float32 [768], P(('dp', 'fsdp'))
- grad_b_output: float32 [768], P(('dp', 'fsdp'))
- grad_b_inner: float32 [3072], P(('dp', 'fsdp'))
- grad_b_outer: float32 [768], P(('dp', 'fsdp'))
- grad_attn_gain: float32 [768], P(('dp', 'fsdp'))
- grad_attn_shift: float32 [768], P(('dp', 'fsdp'))
- grad_ffn_gain: float32 [768], P(('dp', 'fsdp'))
- grad_ffn_shift: float32 [768], P(('dp', 'fsdp'))
- grad_rel_gain: float32 [768], P(('dp', 'fsdp'))
- grad_rel_shift: float32 [768], P(('dp', 'fsdp'))
The draws below stay inside these ranges and needn't reach their ends.
Inputs may be any that keep to these rules, and one draw needn't show every extreme that they name: `routes`: entry k of a row gives t * 2 + p: page k of that device's micro-batch goes to slot p of the bin of fsdp index t in the same dp group and micro-batch. Within a dp group and micro-batch every value occurs once, and a device sends at most one page of a micro-batch to any device. Each row is the lengths of the 3 sequences of one bin, in order, summing to 128. `buckets`: entry 127 + d is the bucket of the distance d.
All inputs are finite; a program needn't handle non-finite values.
Results may differ from the reference program's by a relative error of at most 0.02.
Values may be sent and summed in bfloat16 or wider, within the bound.
No kernel may reach another device: no remote copies, remote signals or barrier semaphores. Data moves between devices by JAX's collectives and lax.ppermute only.
A program may use at most 192 MiB of HBM per device.

```python
import math
import jax
import jax.numpy as jnp
import numpy as np
from jax import lax

D = 768
HEADS = 12
HEAD = 64
FF = 3072
POS = 256
TOK_DEV = 128
MICRO = 2
SEQS = 3
PAGE = 64
PAGES = 2
BINS = 64
TOKENS = 8192
N_DP = 4
N_FSDP = 8


def draw_routes(key, part):
    groups = N_FSDP

    def one_group(subkey):
        first_key, second, third_key = jax.random.split(subkey, 3)
        offsets = jax.random.permutation(first_key, groups)[:PAGES]
        relabel = jax.random.permutation(second, groups)
        slot_keys = jax.random.split(third_key, groups)
        slot_table = jax.vmap(lambda slot_key: jax.random.permutation(slot_key, PAGES))(slot_keys)
        source = jnp.arange(groups, dtype=jnp.int32)[:, None]
        target = relabel[(source + offsets[None, :]) % groups]
        column = jnp.broadcast_to(jnp.arange(PAGES, dtype=jnp.int32)[None, :], (groups, PAGES))
        slot_values = slot_table[target, column]
        return (target * PAGES + slot_values).astype(jnp.int32)
    subkeys = jax.random.split(key, N_DP * MICRO)
    routing = jax.vmap(one_group)(subkeys)
    routing = routing.reshape(N_DP, MICRO, groups, PAGES).transpose(0, 2, 1, 3)
    return routing.reshape(N_DP * groups * MICRO, PAGES)


def plant(values, rng, least, largest):
    longest = values.shape.index(max(values.shape))
    spots = []
    for shift in (0, 1):
        where = [jax.random.randint(jax.random.fold_in(rng, axis), (), 0, length) for axis, length in enumerate(values.shape)]
        where[longest] = (where[longest] + shift) % values.shape[longest]
        spots.append(tuple(where))
    return values.at[spots[0]].set(least).at[spots[1]].set(largest)


def steps_of(own_key, extent, pieces, low, high):
    factor_of, own = 1.0, jax.random.fold_in(own_key, 6)
    for axis_at, parts in pieces:
        steps = jnp.exp(jax.random.uniform(jax.random.fold_in(own, axis_at), (parts,), jnp.float32, low / len(pieces), high / len(pieces)))
        factor_of = factor_of * jnp.repeat(steps, extent[axis_at] // parts).reshape([-1 if axis == axis_at else 1 for axis in range(len(extent))])
    return factor_of


def profile(amount, total, reach, skew):
    weights = [(1 << 20) // math.isqrt(grade ** skew) + 1 for grade in range(2, amount + 1)]
    rest, given = total - reach - (amount - 1), [1] * (amount - 1)
    while rest > 0:
        free = [i for i in range(amount - 1) if given[i] < reach]
        whole, remaining = sum([weights[i] for i in free]), rest
        for i in free:
            addition = min(reach - given[i], max(1, remaining * weights[i] // whole), rest)
            given[i] = given[i] + addition
            rest = rest - addition
    return np.array([reach] + given)


def ragged_sizes(rng, amount, total, reach, lean):
    if amount == 2:
        one = jax.random.randint(rng, (), max(1, total - reach), min(reach, total - 1) + 1)
        return jnp.stack([one, total - one])
    sizes = jnp.asarray(profile(amount, total, reach, lean), jnp.int32)
    couples = (amount - 1) // 2
    giver, sink = sizes[1:1 + 2 * couples:2], sizes[2:2 + 2 * couples:2]
    slack = jnp.minimum(giver - 1, reach - sink)
    shifted = jax.random.randint(jax.random.fold_in(rng, 1), (couples,), 0, 1 << 20) % (slack + 1)
    sizes = sizes.at[1:1 + 2 * couples:2].set(giver - shifted).at[2:2 + 2 * couples:2].set(sink + shifted)
    return sizes[jax.random.permutation(jax.random.fold_in(rng, 2), amount)]


def noise(stream_key, dims, width, limit, pieces=(), kind=jnp.bfloat16):
    values = jax.random.normal(stream_key, dims, jnp.float32) * width
    if len(pieces) > 0:
        values = steps_of(stream_key, dims, pieces, -0.22, 0.18) * values
    return jnp.clip(values, min=-limit, max=limit).astype(kind)


def setup_inputs(seed: int = 0) -> dict:
    streams_of = jax.random.split(jax.random.key(seed), 25)
    return {
        "tokens": noise(streams_of[0], (TOKENS, D), 1.0, 6.0, ((0, 32),)),
        "cotangent": noise(streams_of[1], (TOKENS, D), 1.0, 6.0, ((0, 32),)),
        "routes": draw_routes(jax.random.fold_in(streams_of[24], 71), 0),
        "lengths": jax.vmap(lambda own: ragged_sizes(own, SEQS, TOK_DEV, TOK_DEV // 2, 2))(jax.random.split(streams_of[3], BINS)).reshape((BINS, SEQS)).astype(jnp.int32),
        "buckets": plant(jax.random.randint(streams_of[4], (2 * TOK_DEV - 1,), 0, 2 * POS), jax.random.fold_in(streams_of[4], 1), 0, (2 * POS) - 1).astype(jnp.int32),
        "w_query": noise(streams_of[5], (D, D), D ** -0.5, 0.21875, ((0, 32),)),
        "w_key": noise(streams_of[6], (D, D), D ** -0.5, 0.21875, ((0, 32),)),
        "w_value": noise(streams_of[7], (D, D), D ** -0.5, 0.21875, ((0, 32),)),
        "w_output": noise(streams_of[8], (D, D), (D // 32) ** -0.5, 1.25, ((0, 32),)),
        "w_inner": noise(streams_of[9], (D, FF), D ** -0.5, 0.21875, ((0, 32),)),
        "w_outer": noise(streams_of[10], (FF, D), FF ** -0.5, 0.109375, ((0, 32),)),
        "relative": noise(streams_of[11], (2 * POS, D), 1.0, 6.0, ((0, 32),)),
        "b_query": noise(streams_of[12], (D,), 0.1, 0.59765625, ((0, 32),)),
        "b_key": noise(streams_of[13], (D,), 0.1, 0.59765625, ((0, 32),)),
        "b_value": noise(streams_of[14], (D,), 0.1, 0.59765625, ((0, 32),)),
        "b_output": noise(streams_of[15], (D,), 0.1, 0.59765625, ((0, 32),)),
        "b_inner": noise(streams_of[16], (FF,), 0.1, 0.59765625, ((0, 32),)),
        "b_outer": noise(streams_of[17], (D,), 0.1, 0.59765625, ((0, 32),)),
        "attn_gain": jnp.clip(1.0 + 0.1 * jax.random.normal(streams_of[18], (D,), jnp.float32), 0.5, 1.5).astype(jnp.bfloat16),
        "attn_shift": noise(streams_of[19], (D,), 0.1, 0.59765625, ((0, 32),)),
        "ffn_gain": jnp.clip(1.0 + 0.1 * jax.random.normal(streams_of[20], (D,), jnp.float32), 0.5, 1.5).astype(jnp.bfloat16),
        "ffn_shift": noise(streams_of[21], (D,), 0.1, 0.59765625, ((0, 32),)),
        "rel_gain": jnp.clip(1.0 + 0.1 * jax.random.normal(streams_of[22], (D,), jnp.float32), 0.5, 1.5).astype(jnp.bfloat16),
        "rel_shift": noise(streams_of[23], (D,), 0.1, 0.59765625, ((0, 32),)),
    }


@jax.custom_vjp
def low(v):
    return lax.optimization_barrier(v.astype(jnp.bfloat16)).astype(jnp.float32)

@jax.custom_vjp
def low_back(v):
    return v

def low_keep(v):
    return (low(v), None)

def low_pass(kept, grad):
    return (grad,)

def back_keep(v):
    return (v, None)

def back_low(kept, grad):
    return (low(grad),)
low.defvjp(low_keep, low_pass)
low_back.defvjp(back_keep, back_low)
EPS = 1e-07
UPPER_PRECISION = lax.Precision.HIGHEST
ROOT_HALF = 0.7071067811865476

def round_two(value):
    return low(low_back(value))

def product(left, right):
    return jnp.dot(left, right, precision=UPPER_PRECISION)

def normalize(value, gain, shift):
    average = lax.optimization_barrier(jnp.mean(value, axis=-1, keepdims=True))
    centered = value - average
    spread = lax.optimization_barrier(jnp.mean(centered * centered, axis=-1, keepdims=True))
    return centered * lax.rsqrt(spread + EPS) * gain + shift

def gelu_exact(value):
    return 0.5 * value * (1.0 + lax.erf(value * ROOT_HALF))

def layer_bin(params, inputs, seq_lens, buckets):
    w_query, w_key, w_value, w_output, w_inner, w_outer, relative, b_query, b_key, b_value, b_output, b_inner, b_outer, attn_gain, attn_shift, ffn_gain, ffn_shift, rel_gain, rel_shift = params
    rows_bin = inputs.shape[0]
    score_scale = (3.0 * HEAD) ** (-0.5)
    rel_low = low(normalize(relative, rel_gain, rel_shift))
    query_rows = round_two(product(inputs, w_query) + b_query).reshape(rows_bin, HEADS, HEAD)
    keyed = round_two(product(inputs, w_key) + b_key).reshape(rows_bin, HEADS, HEAD)
    valued = round_two(product(inputs, w_value) + b_value).reshape(rows_bin, HEADS, HEAD)
    pos_query = round_two(product(rel_low, w_query) + b_query).reshape(2 * POS, HEADS, HEAD)
    position_key = round_two(product(rel_low, w_key) + b_key).reshape(2 * POS, HEADS, HEAD)
    position = jnp.arange(rows_bin).astype(jnp.int32)
    distance = (position[:, None] - position[None, :] + (rows_bin - 1)).astype(jnp.int32)
    bucket_idx = buckets[distance].astype(jnp.int32)
    boundary = jnp.cumsum(seq_lens)[:-1]
    segment = lax.optimization_barrier(jnp.sum((position[:, None] >= boundary[None, :]).astype(jnp.int32), axis=1))
    same_seq = segment[:, None] == segment[None, :]
    score_shape = (HEADS, rows_bin, rows_bin)
    content = jnp.einsum('ihd,jhd->hij', query_rows, keyed, precision=UPPER_PRECISION)
    content_position_score = low_back(jnp.einsum('tsk,nsk->stn', query_rows, position_key, precision=UPPER_PRECISION))
    pos_cont = low_back(jnp.einsum('jhd,bhd->hjb', keyed, pos_query, precision=UPPER_PRECISION))
    to_pos = jnp.take_along_axis(content_position_score, jnp.broadcast_to(bucket_idx[None], score_shape), axis=2)
    to_cont = jnp.take_along_axis(pos_cont, jnp.broadcast_to(bucket_idx[None], score_shape), axis=2)
    scores = low_back(score_scale * (content + to_pos + jnp.swapaxes(to_cont, 1, 2)))
    masked = jnp.where(same_seq[None], scores, -1e+30)
    attn_prob = jax.nn.softmax(masked, axis=-1)
    context = jnp.einsum('hij,jhd->ihd', low(attn_prob), valued, precision=UPPER_PRECISION)
    context = round_two(context.reshape(rows_bin, D))
    attended = low_back(product(context, w_output) + b_output)
    hidden = normalize(attended + inputs, attn_gain, attn_shift)
    inner_pre = low_back(product(low(hidden), w_inner) + b_inner)
    outer_out = low_back(product(low(gelu_exact(inner_pre)), w_outer) + b_outer)
    return normalize(outer_out + hidden, ffn_gain, ffn_shift)

def reference(tokens, cotangent, routes, lengths, buckets, w_query, w_key, w_value, w_output, w_inner, w_outer, relative, b_query, b_key, b_value, b_output, b_inner, b_outer, attn_gain, attn_shift, ffn_gain, ffn_shift, rel_gain, rel_shift):
    weights = tuple((item.astype(jnp.float32) for item in (w_query, w_key, w_value, w_output, w_inner, w_outer, relative, b_query, b_key, b_value, b_output, b_inner, b_outer, attn_gain, attn_shift, ffn_gain, ffn_shift, rel_gain, rel_shift)))
    groups = N_FSDP
    slot_count = groups * PAGES
    order = routes.reshape(N_DP, groups, MICRO, PAGES).transpose(0, 2, 1, 3).reshape(N_DP * MICRO, slot_count)
    sizes_bin = lengths.reshape(N_DP, groups, MICRO, SEQS).transpose(0, 2, 1, 3).reshape(N_DP * MICRO * groups, SEQS)

    def to_pages(array):
        shaped = array.reshape(N_DP, groups, MICRO, PAGES, PAGE, D).transpose(0, 2, 1, 3, 4, 5)
        return shaped.reshape(N_DP * MICRO, slot_count, PAGE, D)

    def from_pages(array):
        shaped = array.reshape(N_DP, MICRO, groups, PAGES, PAGE, D).transpose(0, 2, 1, 3, 4, 5)
        return shaped.reshape(TOKENS, D)

    def forward(params, inputs):
        pages_all = to_pages(inputs)
        placed = jax.vmap(lambda page_set, order_row: jnp.zeros_like(page_set).at[order_row].set(page_set))(pages_all, order)
        bins_all = placed.reshape(N_DP * MICRO * groups, TOK_DEV, D)
        stepper = jax.checkpoint(lambda bin_pair: layer_bin(params, bin_pair[0], bin_pair[1], buckets))
        results = lax.map(stepper, (bins_all, sizes_bin))
        results = results.reshape(N_DP * MICRO, slot_count, PAGE, D)
        returned = jax.vmap(lambda page_set, order_row: page_set[order_row])(results, order)
        return from_pages(returned)
    inputs_wide = tokens.astype(jnp.float32)
    result, pullback = jax.vjp(forward, weights, inputs_wide)
    grads, grad_in = pullback(cotangent.astype(jnp.float32))
    return (result.astype(jnp.bfloat16), grad_in.astype(jnp.bfloat16), grads[0], grads[1], grads[2], grads[3], grads[4], grads[5], grads[6], grads[7], grads[8], grads[9], grads[10], grads[11], grads[12], grads[13], grads[14], grads[15], grads[16], grads[17], grads[18])
```

```python
import jax
import jax.numpy as jnp
from jax import lax
from jax.experimental import pallas as pl
from jax.experimental.pallas import tpu as pltpu
from jax.sharding import PartitionSpec as P

HEADS = 12
HEAD = 64
POS = 256
MICRO = 2
PAGE = 64
VECS = 16

EPS = 1e-07
ROOT_HALF = 0.7071067811865476
ROOT_TWO_PI = 2.5066282746310002
SCALE = (3.0 * HEAD) ** (-0.5)
ALL = ("dp", "fsdp")
F32 = jnp.float32
BF16 = jnp.bfloat16

B_QUERY, B_KEY, B_VALUE, B_OUTPUT, B_OUTER = 0, 1, 2, 3, 4
ATTN_GAIN, ATTN_SHIFT, FFN_GAIN, FFN_SHIFT, REL_GAIN, REL_SHIFT, B_INNER = 5, 6, 7, 8, 9, 10, 11


def dot(left, right):
    return jnp.dot(left, right, preferred_element_type=F32)


def dot_tn(left, right):
    return lax.dot_general(left, right, (((0,), (0,)), ((), ())), preferred_element_type=F32)


def dot_nt(left, right):
    return lax.dot_general(left, right, (((1,), (1,)), ((), ())), preferred_element_type=F32)


def column_sum(value):
    return jnp.sum(value.astype(F32), axis=0, keepdims=True)


def normalize(value):
    centered = value - jnp.mean(value, axis=-1, keepdims=True)
    inv_dev = lax.rsqrt(jnp.mean(centered * centered, axis=-1, keepdims=True) + EPS)
    return centered * inv_dev, inv_dev


def normalize_back(grad_out, unit, inv_dev, gain):
    scaled = grad_out * gain
    mixed = scaled - jnp.mean(scaled, axis=-1, keepdims=True)
    mixed = mixed - unit * jnp.mean(scaled * unit, axis=-1, keepdims=True)
    return mixed * inv_dev


def one_hot_rows(bucket_ref, count):
    rows = bucket_ref.shape[0]
    return (bucket_ref[...] == lax.broadcasted_iota(jnp.int32, (rows, count), 1)).astype(BF16)


def skewed(dist):
    rows = dist.shape[0]
    return pltpu.roll(dist, rows + 1, 1, stride=1, stride_axis=0)[:, :rows]


def attention_forward(
    x_ref, wq_ref, wk_ref, wv_ref, rel_ref, vec_ref, bucket_ref, seg_col_ref, seg_row_ref,
    q_ref, k_ref, v_ref, pq_ref, pk_ref, rel_low_ref, prob_ref, context_ref,
):
    rows = seg_row_ref.shape[1]
    bins = seg_row_ref.shape[0]
    pair = 2 * HEAD
    x = x_ref[...]
    vec = vec_ref[...].astype(F32)
    row = lambda at: vec[at : at + 1]
    q_ref[...] = (dot(x, wq_ref[...]) + row(B_QUERY)).astype(BF16)
    k_ref[...] = (dot(x, wk_ref[...]) + row(B_KEY)).astype(BF16)
    v_ref[...] = (dot(x, wv_ref[...]) + row(B_VALUE)).astype(BF16)
    unit, _ = normalize(dot(one_hot_rows(bucket_ref, rel_ref.shape[0]), rel_ref[...]))
    rel_low = (unit * row(REL_GAIN) + row(REL_SHIFT)).astype(BF16)
    rel_low_ref[...] = rel_low
    pq_ref[...] = (dot(rel_low, wq_ref[...]) + row(B_QUERY)).astype(BF16)
    pk_ref[...] = (dot(rel_low, wk_ref[...]) + row(B_KEY)).astype(BF16)
    first = lax.broadcasted_iota(jnp.int32, (rows, pair), 1) < HEAD
    firsts = lax.broadcasted_iota(jnp.int32, (bins * rows, pair), 1) < HEAD
    same = [
        seg_col_ref[b * rows : (b + 1) * rows, :] == seg_row_ref[b : b + 1, :] for b in range(bins)
    ]

    def body(step, carry):
        lanes = pl.ds(pl.multiple_of(step * pair, pair), pair)
        q, k, v = q_ref[:, lanes], k_ref[:, lanes], v_ref[:, lanes]
        pq, pk = pq_ref[:, lanes], pk_ref[:, lanes]
        parts = [[None] * 2 for _ in range(bins)]
        for h in range(2):
            own = firsts if h == 0 else jnp.logical_not(firsts)
            qh = jnp.where(own, q, jnp.zeros_like(q))
            kh = jnp.where(own, k, jnp.zeros_like(k))
            to_pos = dot_nt(qh, pk)
            to_cont = dot_nt(kh, pq)
            for b in range(bins):
                at = slice(b * rows, (b + 1) * rows)
                scores = dot_nt(qh[at], k[at]) + skewed(to_pos[at]) + skewed(to_cont[at]).T
                masked = jnp.where(same[b], SCALE * scores, -1e30)
                power = jnp.exp(masked - jnp.max(masked, axis=-1, keepdims=True))
                prob = power / jnp.sum(power, axis=-1, keepdims=True)
                prob_ref[(step * 2 + h) * bins + b] = prob
                parts[b][h] = dot(prob.astype(BF16), v[at])
        for b in range(bins):
            context_ref[b * rows : (b + 1) * rows, lanes] = jnp.where(
                first, parts[b][0], parts[b][1]
            ).astype(BF16)
        return carry

    lax.fori_loop(0, HEADS // 2, body, 0)


def ffn_forward(
    context_ref, x_ref, wo_ref, wi_ref, wout_ref, vec_ref, cot_ref,
    result_ref, unit_one_ref, inv_one_ref, hidden_low_ref, slope_ref, grad_res_ref, grad_outer_ref,
    grad_wout_ref, sums_ref,
):
    chunks = wi_ref.shape[0]
    vec = vec_ref[...].astype(F32)
    row = lambda at: vec[at : at + 1]
    attended = dot(context_ref[...], wo_ref[...]) + row(B_OUTPUT)
    unit, inv = normalize(attended + x_ref[...].astype(F32))
    unit_one_ref[...] = unit
    inv_one_ref[...] = inv
    hidden = unit * row(ATTN_GAIN) + row(ATTN_SHIFT)
    hidden_low = hidden.astype(BF16)
    hidden_low_ref[...] = hidden_low
    total = hidden + row(B_OUTER)
    active = []
    for c in range(chunks):
        inner = dot(hidden_low, wi_ref[c]) + row(B_INNER + c)
        phi = 0.5 * (1.0 + lax.erf(inner * ROOT_HALF))
        slope_ref[c] = phi + inner * jnp.exp(-0.5 * inner * inner) / ROOT_TWO_PI
        active.append((inner * phi).astype(BF16))
        total = total + dot(active[c], wout_ref[c])
    unit, inv = normalize(total)
    result_ref[...] = (unit * row(FFN_GAIN) + row(FFN_SHIFT)).astype(BF16)
    cot = cot_ref[...].astype(F32)
    grad_res = normalize_back(cot, unit, inv, row(FFN_GAIN))
    grad_res_ref[...] = grad_res
    grad_outer = grad_res.astype(BF16)
    grad_outer_ref[...] = grad_outer
    sums_ref[...] = jnp.concatenate(
        [column_sum(grad_outer), column_sum(cot * unit), column_sum(cot)]
        + [jnp.zeros_like(cot[:1])] * 5,
        axis=0,
    )
    for c in range(chunks):
        grad_wout_ref[c] = dot_tn(active[c], grad_outer).astype(BF16)


def ffn_backward(
    grad_outer_ref, grad_res_ref, slope_ref, hidden_low_ref, unit_one_ref, inv_one_ref, context_ref,
    wo_ref, wi_ref, wout_ref, vec_ref,
    grad_wi_ref, grad_wo_ref, grad_one_ref, grad_context_ref, sums_ref,
):
    chunks = wi_ref.shape[0]
    vec = vec_ref[...].astype(F32)
    row = lambda at: vec[at : at + 1]
    grad_outer = grad_outer_ref[...]
    hidden_low = hidden_low_ref[...]
    grad_hidden = grad_res_ref[...]
    bias = []
    for c in range(chunks):
        grad_inner = (dot_nt(grad_outer, wout_ref[c]) * slope_ref[c]).astype(BF16)
        grad_wi_ref[c] = dot_tn(hidden_low, grad_inner).astype(BF16)
        bias.append(column_sum(grad_inner))
        grad_hidden = grad_hidden + dot_nt(grad_inner, wi_ref[c])
    unit = unit_one_ref[...]
    grad_one = normalize_back(grad_hidden, unit, inv_one_ref[...], row(ATTN_GAIN))
    grad_one_ref[...] = grad_one
    grad_att = grad_one.astype(BF16)
    sums_ref[...] = jnp.concatenate(
        bias
        + [column_sum(grad_att), column_sum(grad_hidden * unit), column_sum(grad_hidden)]
        + [jnp.zeros_like(bias[0])] * (5 - chunks),
        axis=0,
    )
    grad_context_ref[...] = dot_nt(grad_att, wo_ref[...]).astype(BF16)
    grad_wo_ref[...] = dot_tn(context_ref[...], grad_att).astype(BF16)


def attention_backward(
    grad_context_ref, grad_one_ref, x_ref, q_ref, k_ref, v_ref, pq_ref, pk_ref, rel_low_ref, prob_ref,
    wq_ref, wk_ref, wv_ref, rel_ref, vec_ref, bucket_ref,
    grad_wq_ref, grad_wk_ref, grad_wv_ref, grad_rel_ref, grad_in_ref, sums_ref,
    dq_ref, dk_ref, dv_ref, dpq_ref, dpk_ref, qf_ref, kf_ref,
):
    bins = prob_ref.shape[0] // HEADS
    rows = prob_ref.shape[1]
    pair = 2 * HEAD
    first = lax.broadcasted_iota(jnp.int32, (rows, pair), 1) < HEAD
    firsts = lax.broadcasted_iota(jnp.int32, (2 * rows, pair), 1) < HEAD
    flip = (
        lax.broadcasted_iota(jnp.int32, (rows, rows), 0)
        + lax.broadcasted_iota(jnp.int32, (rows, rows), 1)
        == rows - 1
    ).astype(BF16)
    for b in range(bins):
        at = slice(b * rows, (b + 1) * rows)
        qf_ref[at, :] = dot(flip, q_ref[at, :]).astype(BF16)
        kf_ref[at, :] = dot(flip, k_ref[at, :]).astype(BF16)

    def unskewed(square):
        wide = jnp.concatenate([square, jnp.zeros_like(square)], axis=1)
        return pltpu.roll(wide, 0, 1, stride=1, stride_axis=0).astype(BF16)

    def unflip(value):
        high = value.astype(BF16)
        return dot(flip, high) + dot(flip, (value - high.astype(F32)).astype(BF16))

    def body(step, carry):
        lanes = pl.ds(pl.multiple_of(step * pair, pair), pair)
        q, k, v = q_ref[:, lanes], k_ref[:, lanes], v_ref[:, lanes]
        pq, pk = pq_ref[:, lanes], pk_ref[:, lanes]
        qf, kf, dc = qf_ref[:, lanes], kf_ref[:, lanes], grad_context_ref[:, lanes]
        dpq, dpk = [], []
        grads = [[None] * 2 for _ in range(bins)]
        for h in range(2):
            own = first if h == 0 else jnp.logical_not(first)
            to_pos, to_cont = [], []
            for b in range(bins):
                at = slice(b * rows, (b + 1) * rows)
                prob = prob_ref[(step * 2 + h) * bins + b]
                dch = jnp.where(own, dc[at], jnp.zeros_like(dc[at]))
                grad_prob = dot_nt(dch, v[at])
                dv = dot_tn(prob.astype(BF16), dc[at])
                dots = jnp.sum(prob * grad_prob, axis=-1, keepdims=True)
                score = (prob * (grad_prob - dots)).astype(BF16)
                by_pos = unskewed(dot(flip, score))
                by_cont = unskewed(dot_nt(flip, score))
                to_pos.append(by_pos)
                to_cont.append(by_cont)
                dq = dot(score, k[at]) + unflip(dot(by_pos, pk))
                dk = dot_tn(score, q[at]) + unflip(dot(by_cont, pq))
                grads[b][h] = (dq, dk, dv)
            dpk.append(dot_tn(jnp.concatenate(to_pos, axis=0), qf))
            dpq.append(dot_tn(jnp.concatenate(to_cont, axis=0), kf))
        for b in range(bins):
            at = slice(b * rows, (b + 1) * rows)
            (dq0, dk0, dv0), (dq1, dk1, dv1) = grads[b]
            dq_ref[at, lanes] = (SCALE * jnp.where(first, dq0, dq1)).astype(BF16)
            dk_ref[at, lanes] = (SCALE * jnp.where(first, dk0, dk1)).astype(BF16)
            dv_ref[at, lanes] = jnp.where(first, dv0, dv1).astype(BF16)
        dpq_ref[:, lanes] = (SCALE * jnp.where(firsts, dpq[0], dpq[1])).astype(BF16)
        dpk_ref[:, lanes] = (SCALE * jnp.where(firsts, dpk[0], dpk[1])).astype(BF16)
        return carry

    lax.fori_loop(0, HEADS // 2, body, 0)
    vec = vec_ref[...].astype(F32)
    x, rel_low = x_ref[...], rel_low_ref[...]
    dq, dk, dv, dpq, dpk = dq_ref[...], dk_ref[...], dv_ref[...], dpq_ref[...], dpk_ref[...]
    grad_wq_ref[...] = (dot_tn(x, dq) + dot_tn(rel_low, dpq)).astype(BF16)
    grad_wk_ref[...] = (dot_tn(x, dk) + dot_tn(rel_low, dpk)).astype(BF16)
    grad_wv_ref[...] = dot_tn(x, dv).astype(BF16)
    wq, wk = wq_ref[...], wk_ref[...]
    grad_in_ref[...] = (
        grad_one_ref[...] + dot_nt(dq, wq) + dot_nt(dk, wk) + dot_nt(dv, wv_ref[...])
    ).astype(BF16)
    choose = one_hot_rows(bucket_ref, rel_ref.shape[0])
    unit, inv = normalize(dot(choose, rel_ref[...]))
    grad_low = dot_nt(dpq, wq) + dot_nt(dpk, wk)
    grad_rel = normalize_back(grad_low, unit, inv, vec[REL_GAIN : REL_GAIN + 1])
    high = grad_rel.astype(BF16)
    low = (grad_rel - high.astype(F32)).astype(BF16)
    grad_rel_ref[...] = (dot_tn(choose, high) + dot_tn(choose, low)).astype(BF16)
    sums_ref[...] = jnp.concatenate(
        [
            column_sum(dq) + column_sum(dpq),
            column_sum(dk) + column_sum(dpk),
            column_sum(dv),
            column_sum(grad_low * unit),
            column_sum(grad_low),
        ]
        + [jnp.zeros_like(grad_low[:1])] * 3,
        axis=0,
    )


def kernel_call(body, name, outs, scratch=(), flops=0, moved=0):
    space = pl.BlockSpec(memory_space=pltpu.VMEM)

    def call(*args):
        return pl.pallas_call(
            body,
            name=name,
            out_shape=[jax.ShapeDtypeStruct(shape, kind) for shape, kind in outs],
            in_specs=[space] * len(args),
            out_specs=[space] * len(outs),
            scratch_shapes=list(scratch),
            cost_estimate=pl.CostEstimate(flops=flops, bytes_accessed=moved, transcendentals=0),
        )(*args)

    return call


def on_device(
    tokens, cotangent, routes, lengths, buckets,
    w_query, w_key, w_value, w_output, w_inner, w_outer, relative,
    b_query, b_key, b_value, b_output, b_inner, b_outer,
    attn_gain, attn_shift, ffn_gain, ffn_shift, rel_gain, rel_shift,
):
    groups = lax.axis_size("fsdp")
    count = lax.axis_size("dp") * groups
    seat = lax.axis_index("fsdp")
    me = lax.axis_index("dp") * groups + seat
    both, width = tokens.shape
    rows = both // MICRO
    pages = rows // PAGE
    unit = width // count
    wide = w_inner.shape[1] // width
    dist = 2 * rows

    singles = jnp.stack(
        [b_query, b_key, b_value, b_output, b_outer, attn_gain, attn_shift, ffn_gain, ffn_shift,
         rel_gain, rel_shift]
    )
    zero = jnp.zeros((), jnp.int32)
    placed = lax.dynamic_update_slice(
        jnp.zeros((singles.shape[0], width), BF16), singles, (zero, me * unit)
    )
    inner_placed = lax.dynamic_update_slice(
        jnp.zeros((wide * width,), BF16), b_inner, (me * b_inner.shape[0],)
    ).reshape(wide, width)
    vec_part = jnp.concatenate(
        [placed, inner_placed, jnp.zeros((VECS - singles.shape[0] - wide, width), BF16)], axis=0
    )
    inner_part = w_inner.reshape(unit, wide, width).transpose(1, 0, 2).reshape(unit * wide, width)
    pack = jnp.concatenate(
        [w_query, w_key, w_value, relative, vec_part, w_output, inner_part, w_outer], axis=0
    )
    full = lax.all_gather(pack, ALL, axis=0, tiled=False)
    cuts = [0]
    for part in (w_query, w_key, w_value, relative, vec_part, w_output, inner_part, w_outer):
        cuts.append(cuts[-1] + part.shape[0])
    piece = lambda at: full[:, cuts[at] : cuts[at + 1]]
    wq, wk, wv, rel = [piece(at).reshape(-1, width) for at in range(4)]
    vec = jnp.sum(piece(4).astype(F32), axis=0)
    wo = piece(5).reshape(-1, width)
    wi = piece(6).reshape(count, wide, unit, width).transpose(1, 0, 2, 3).reshape(wide, width, width)
    wout = piece(7).reshape(wide, width, width)

    table = lax.all_gather(routes, "fsdp", axis=0, tiled=False)
    target = routes // pages
    pick = (target[:, None, :] == jnp.arange(groups, dtype=jnp.int32)[None, :, None]).astype(BF16)
    slots = seat * pages + jnp.arange(pages, dtype=jnp.int32)
    place = jnp.any(
        table.transpose(1, 0, 2)[:, None, :, :] == slots[None, :, None, None], axis=3
    ).astype(BF16)
    own = jnp.stack([tokens, cotangent]).reshape(2, MICRO, pages, PAGE * width)
    send = jnp.einsum("mgk,amkr->gamr", pick, own, preferred_element_type=F32).astype(BF16)
    got = lax.all_to_all(send, "fsdp", split_axis=0, concat_axis=0, tiled=True)
    binned = jnp.einsum("mps,samr->ampr", place, got, preferred_element_type=F32).astype(BF16)
    binned = binned.reshape(2, both, width)
    x, cot = binned[0], binned[1]

    bounds = jnp.cumsum(lengths, axis=1)[:, :-1]
    segment = jnp.sum(
        (jnp.arange(rows, dtype=jnp.int32)[None, :, None] >= bounds[:, None, :]).astype(jnp.int32),
        axis=2,
    )
    bucket_col = jnp.concatenate([jnp.flip(buckets), jnp.full((1,), -1, jnp.int32)])[:, None]

    low = (both, width)
    q, k, v, pq, pk, rel_low, prob, context = kernel_call(
        attention_forward, "attention_forward",
        [(low, BF16)] * 3 + [((dist, width), BF16)] * 3
        + [((MICRO * HEADS, rows, rows), F32), (low, BF16)],
    )(x, wq, wk, wv, rel, vec, bucket_col, segment.reshape(both, 1), segment)
    result, unit_one, inv_one, hidden_low, slope, grad_res, grad_outer, grad_wout, sums_a = kernel_call(
        ffn_forward, "ffn_forward",
        [(low, BF16), (low, F32), ((both, 1), F32), (low, BF16), ((wide,) + low, F32), (low, F32),
         (low, BF16), ((wide, width, width), BF16), ((8, width), F32)],
    )(context, x, wo, wi, wout, vec, cot)
    grad_wi, grad_wo, grad_one, grad_context, sums_b = kernel_call(
        ffn_backward, "ffn_backward",
        [((wide, width, width), BF16), ((width, width), BF16), (low, F32), (low, BF16),
         ((8, width), F32)],
    )(grad_outer, grad_res, slope, hidden_low, unit_one, inv_one, context, wo, wi, wout, vec)
    grad_wq, grad_wk, grad_wv, grad_rel, grad_in, sums_c = kernel_call(
        attention_backward, "attention_backward",
        [((width, width), BF16)] * 3 + [(rel.shape, BF16), (low, BF16), ((8, width), F32)],
        [pltpu.VMEM(low, BF16)] * 3 + [pltpu.VMEM((dist, width), BF16)] * 2
        + [pltpu.VMEM(low, BF16)] * 2,
    )(grad_context, grad_one, x, q, k, v, pq, pk, rel_low, prob, wq, wk, wv, rel, vec, bucket_col)

    sums = jnp.concatenate([sums_a, sums_b, sums_c], axis=0).astype(BF16)
    sent = jnp.concatenate(
        [
            grad_wq.reshape(count, -1, width),
            grad_wk.reshape(count, -1, width),
            grad_wv.reshape(count, -1, width),
            grad_rel.reshape(count, -1, width),
            jnp.broadcast_to(sums[None], (count,) + sums.shape),
            grad_wo.reshape(count, -1, width),
            grad_wi.reshape(wide, count, unit, width).transpose(1, 0, 2, 3).reshape(count, -1, width),
            grad_wout.reshape(count, -1, width),
        ],
        axis=1,
    )
    mine = lax.psum_scatter(sent, ALL, scatter_dimension=0, tiled=False).astype(F32)
    ends = [0]
    for size in (unit, unit, unit, relative.shape[0], sums.shape[0], unit, unit * wide, unit * wide):
        ends.append(ends[-1] + size)
    take = lambda at: mine[ends[at] : ends[at + 1]]
    g_inner = take(6).reshape(wide, unit, width).transpose(1, 0, 2).reshape(unit, wide * width)
    vectors = lax.dynamic_slice(take(4), (zero, me * unit), (sums.shape[0], unit))
    v_inner = lax.dynamic_slice(
        take(4)[8 : 8 + wide].reshape(-1), (me * b_inner.shape[0],), b_inner.shape
    )

    done = jnp.stack([result, grad_in]).reshape(2, MICRO, pages, PAGE * width)
    back = jnp.einsum("mps,ampr->samr", place, done, preferred_element_type=F32).astype(BF16)
    home = lax.all_to_all(back, "fsdp", split_axis=0, concat_axis=0, tiled=True)
    home = jnp.einsum("mgk,gamr->amkr", pick, home, preferred_element_type=F32).astype(BF16)
    home = home.reshape(2, both, width)
    return (
        home[0], home[1], take(0), take(1), take(2), take(5), g_inner, take(7), take(3),
        vectors[16], vectors[17], vectors[18], vectors[8 + wide], v_inner, vectors[0],
        vectors[9 + wide], vectors[10 + wide], vectors[1], vectors[2], vectors[19], vectors[20],
    )


def solution(mesh):
    flat = P(ALL)
    rows = P(ALL, None)
    in_specs = (rows,) * 4 + (P(),) + (rows,) * 7 + (flat,) * 12
    out_specs = (rows,) * 9 + (flat,) * 12
    return jax.shard_map(
        on_device, mesh=mesh, in_specs=in_specs, out_specs=out_specs, check_vma=False
    )
```
